32 devices in a mesh: row: 4 (over y, x), col: 8 (over z, core).
Axes of the slice: x: 2, y: 2, z: 4, core: 2. Of those that a mesh axis runs over, the one named last changes fastest.
Arguments:
- features: bfloat16 [8192, 128], P(('row', 'col')), may hold values from -6 to 6
- weight: bfloat16 [128, 256], replicated, may hold values from -0.5 to 0.5
- cotangent: bfloat16 [8192, 256], P(('row', 'col')), may hold values from -6 to 6
- tile_values: bfloat16 [4, 8, 96, 128, 128], P('row', 'col'), may hold values from -0.3125 to 0.3125
- tile_rows: int32 [4, 8, 96], P('row', 'col'), may hold values from 0 to 15
- tile_cols: int32 [4, 8, 96], P('row', 'col'), may hold values from 0 to 7
- tile_counts: int32 [4, 8], P('row', 'col'), may hold values from 12 to 96, as said below
Outputs:
- output: bfloat16 [8192, 256], P(('row', 'col'))
- grad_features: bfloat16 [8192, 128], P(('row', 'col'))
- grad_weight: float32 [128, 256], replicated
The draws below stay inside these ranges and needn't reach their ends.
Inputs may be any that keep to these rules, and one draw needn't show every extreme that they name: Slots 0 to tile_counts - 1 of a grid cell are live and the rest are ignored; the (row tile, column tile) pairs of a cell's live slots are distinct; some cells hold 96 live slots.
All inputs are finite; a program needn't handle non-finite values.
Results may differ from the reference program's by a relative error of at most 0.0049.
Values may be sent and summed in bfloat16 or wider, within the bound.
A program may use at most 128 MiB of HBM per device.

```python
import jax
import jax.numpy as jnp
from jax import lax

F = 128
H = 256
TILE = 128
NB = 256
GRID_ROWS = 4
GRID_COLS = 8
NODES = 8192
RT = 16
CT = 8
TMAX = 96


def tile_slots(key):
    folded = jax.random.fold_in(key, 7)
    device_keys = jax.random.split(folded, GRID_ROWS * GRID_COLS)

    def one_device(device_key):
        return jax.random.permutation(device_key, RT * CT)[:TMAX]
    slot_ids = jax.vmap(one_device)(device_keys)
    return slot_ids.reshape(GRID_ROWS, GRID_COLS, TMAX).astype(jnp.int32)


def draw_tile_rows(key, part):
    return tile_slots(key) // CT


def draw_tile_cols(key, part):
    return tile_slots(key) % CT


def draw_tile_counts(key, part):
    folded = jax.random.fold_in(key, 11)
    key_counts, key_heavy = jax.random.split(folded)
    counts = jax.random.randint(key_counts, (GRID_ROWS * GRID_COLS,), TMAX // 8, TMAX // 2 + 1)
    heavy_ids = jax.random.permutation(key_heavy, GRID_ROWS * GRID_COLS)[:4]
    counts = counts.at[heavy_ids].set(TMAX)
    return counts.reshape(GRID_ROWS, GRID_COLS).astype(jnp.int32)


def shard_levels(own_key, dims, cuts, smallest, top_value):
    factor_of, own = 1.0, jax.random.fold_in(own_key, 6)
    for axis_at, blocks in cuts:
        heights = jnp.exp(jax.random.uniform(jax.random.fold_in(own, axis_at), (blocks,), jnp.float32, smallest / len(cuts), top_value / len(cuts)))
        factor_of = factor_of * jnp.repeat(heights, dims[axis_at] // blocks).reshape([-1 if axis == axis_at else 1 for axis in range(len(dims))])
    return factor_of


def normal_values(own_key, dims, scale, bound, pieces=(), dtype=jnp.bfloat16):
    entries = scale * jax.random.normal(own_key, dims, jnp.float32)
    if pieces:
        entries = entries * shard_levels(own_key, dims, pieces, -0.22, 0.18)
    return jnp.clip(entries, -bound, bound).astype(dtype)


def setup_inputs(seed: int = 0) -> dict:
    keys = jax.random.split(jax.random.key(seed), 8)
    features = normal_values(keys[0], (NODES, F), 1.0, 6.0, ((0, 32),))
    weight = normal_values(keys[1], (F, H), F ** -0.5, 0.5)
    cotangent = normal_values(keys[2], (NODES, H), 1.0, 6.0, ((0, 32),))
    tile_values = normal_values(keys[3], (GRID_ROWS, GRID_COLS, TMAX, TILE, TILE), ((5 * TILE * GRID_COLS * TMAX / (16 * RT)) ** -0.5), 0.3125, ((0, 4), (1, 8)))
    tile_rows = draw_tile_rows(jax.random.fold_in(keys[7], 71), 0)
    tile_cols = draw_tile_cols(jax.random.fold_in(keys[7], 71), 0)
    tile_counts = draw_tile_counts(jax.random.fold_in(keys[7], 71), 0)
    return {"features": features, "weight": weight, "cotangent": cotangent, "tile_values": tile_values, "tile_rows": tile_rows, "tile_cols": tile_cols, "tile_counts": tile_counts}


def silu_slope(values):
    sigmoid_part = jax.nn.sigmoid(values)
    return sigmoid_part * (1.0 + values * (1.0 - sigmoid_part))


def tile_product(slot_values, slot_rows, slot_cols, live_count, source, out_tiles):
    live_mask = jnp.arange(slot_values.shape[0]) < live_count
    weights = jnp.where(live_mask[:, None, None], slot_values.astype(jnp.float32), jnp.zeros((), jnp.float32))
    picked = jnp.take(source, slot_cols, axis=0).astype(jnp.float32)
    products = jnp.einsum('tij,tjh->tih', weights, picked, precision=lax.Precision.HIGHEST)
    empty = jnp.zeros((out_tiles,) + products.shape[1:], jnp.float32)
    return empty.at[slot_rows].add(products)


def reference(features, weight, cotangent, tile_values, tile_rows, tile_cols, tile_counts):
    blocks = features.reshape(GRID_ROWS, GRID_COLS, NB, F)
    sources = jnp.swapaxes(blocks, 0, 1).reshape(GRID_COLS, CT, TILE, F)

    def forward_row(row_args):
        def add_block(running, block_args):
            block_values, block_rows, block_cols, block_count, block_source = block_args
            return running + tile_product(block_values, block_rows, block_cols, block_count, block_source, RT), None

        running, unused = lax.scan(add_block, jnp.zeros((RT, TILE, F), jnp.float32), tuple(row_args) + (sources,))
        return running

    aggregated = lax.map(forward_row, (tile_values, tile_rows, tile_cols, tile_counts)).reshape(NODES, F)
    summed = jnp.dot(aggregated, weight.astype(jnp.float32), precision=lax.Precision.HIGHEST)
    output = jax.nn.silu(summed).astype(jnp.bfloat16)
    grad_summed = (cotangent.astype(jnp.float32) * silu_slope(summed)).astype(jnp.bfloat16)
    grad_sources = grad_summed.reshape(GRID_ROWS, RT, TILE, H)

    def backward_col(col_index):
        def add_block(running, row_index):
            flipped = jnp.swapaxes(tile_values[row_index, col_index], 1, 2)
            term = tile_product(flipped, tile_cols[row_index, col_index], tile_rows[row_index, col_index], tile_counts[row_index, col_index], grad_sources[row_index], CT)
            return running + term, None

        running, unused = lax.scan(add_block, jnp.zeros((CT, TILE, H), jnp.float32), jnp.arange(GRID_ROWS))
        return running

    grad_cols = lax.map(backward_col, jnp.arange(GRID_COLS))
    grad_mixed = jnp.swapaxes(grad_cols.reshape(GRID_COLS, GRID_ROWS, NB, H), 0, 1).reshape(NODES, H)
    grad_features = jnp.dot(grad_mixed, weight.astype(jnp.float32).T, precision=lax.Precision.HIGHEST).astype(jnp.bfloat16)
    grad_weight = jnp.dot(features.astype(jnp.float32).T, grad_mixed, precision=lax.Precision.HIGHEST) * (NODES ** -0.5)
    return output, grad_features, grad_weight
```

```python
import functools

import jax
import jax.numpy as jnp
from jax import lax
from jax.experimental import pallas as pl
from jax.experimental.pallas import tpu as pltpu
from jax.sharding import PartitionSpec as P

MESH = pl.DeviceIdType.MESH


def dot(a, b):
    return jnp.dot(a, b, preferred_element_type=jnp.float32)


def split_high_low(values):
    high = values.astype(jnp.bfloat16)
    return high, (values - high.astype(jnp.float32)).astype(jnp.bfloat16)


def kernel(rows, cols, sizes, slot_of, feats, weight, cot, tiles, out, grad_feat, grad_weight,
           slots, dense, flipped, feat_all, pair_send, pair_recv, pair_own, hop_send, hop_recv,
           grad_all, acc, row_send, row_recv, w_term, w_row, w_quarter, w_pair, w_hop, w_all,
           load_sem, feat_s, feat_r, pair_s, pair_r, hop_s, hop_r, gp_s, gp_r, gz_s, gz_r, gf_s, gf_r,
           row_s, row_r, w1_s, w1_r, w2_s, w2_r, w3_s, w3_r, w4_s, w4_r):
    block, tile, row_tiles, col_tiles, slot_total = sizes
    chips = cols // 2
    i = lax.axis_index("row")
    j = lax.axis_index("col")
    q = j // 2
    core = j % 2
    other = 1 - core
    partner = (i, 2 * q + other)

    def row_at(step):
        return lax.rem(i + step, rows)

    def chip_at(step):
        return lax.rem(q + step, chips)

    def send(src, dst, ssem, rsem, device):
        copy = pltpu.make_async_remote_copy(
            src_ref=src, dst_ref=dst, send_sem=ssem, recv_sem=rsem, device_id=device, device_id_type=MESH)
        copy.start()
        return copy

    started = []

    load_tiles = pltpu.make_async_copy(tiles, slots.at[pl.ds(0, slot_total)], load_sem.at[0])
    load_tiles.start()
    own_block = pl.ds(pl.multiple_of(i * block, block), block)
    load_feats = pltpu.make_async_copy(feats, feat_all.at[own_block], load_sem.at[1])
    load_feats.start()

    barrier = pltpu.get_barrier_semaphore()
    peers = [partner]
    for d in range(1, rows):
        peers.append((row_at(d), j))
        peers.append((row_at(d), 2 * q + other))
    for d in range(1, chips):
        peers.append((i, 2 * chip_at(d) + core))
    for peer in peers:
        pl.semaphore_signal(barrier, inc=1, device_id=peer, device_id_type=MESH)
    pl.semaphore_wait(barrier, len(peers))

    feat_copies = []
    for d in range(1, rows):
        feat_copies.append(send(feats, feat_all.at[own_block], feat_s.at[d - 1], feat_r.at[d - 1], (row_at(d), j)))

    slots[slot_total] = jnp.zeros((tile, tile), jnp.bfloat16)
    load_tiles.wait()

    def place(r, carry):
        at = pl.ds(pl.multiple_of(r * tile, tile), tile)
        for c in range(col_tiles):
            dense[at, c * tile:(c + 1) * tile] = slots[slot_of[r * col_tiles + c]]
        return carry

    lax.fori_loop(0, row_tiles, place, 0)

    load_feats.wait()
    for copy in feat_copies:
        copy.wait_recv()
    started += feat_copies

    def partial_of(dest):
        return dot(dense[pl.ds(pl.multiple_of(dest * block, block), block), :], feat_all[...])

    order = list(range(1, chips)) + [0]
    pair_copies = {}
    for d in order:
        pair_send[d] = partial_of(2 * chip_at(d) + other).astype(jnp.bfloat16)
        pair_copies[d] = send(pair_send.at[d], pair_recv.at[d], pair_s.at[d], pair_r.at[d], partner)
    hop_copies = []
    for d in order:
        mine = partial_of(2 * chip_at(d) + core)
        pair_copies[d].wait_recv()
        mine = mine + pair_recv[d].astype(jnp.float32)
        if d:
            hop_send[d - 1] = mine.astype(jnp.bfloat16)
            hop_copies.append(send(hop_send.at[d - 1], hop_recv.at[d - 1], hop_s.at[d - 1], hop_r.at[d - 1],
                                   (i, 2 * chip_at(d) + core)))
        else:
            pair_own[...] = mine
    started += list(pair_copies.values()) + hop_copies

    def turn(r, carry):
        at = pl.ds(pl.multiple_of(r * tile, tile), tile)
        for c in range(col_tiles):
            flipped[c * tile:(c + 1) * tile, at] = dense[at, c * tile:(c + 1) * tile].T
        return carry

    lax.fori_loop(0, row_tiles, turn, 0)

    mixed = pair_own[...]
    for d, copy in enumerate(hop_copies):
        copy.wait_recv()
        mixed = mixed + hop_recv[d].astype(jnp.float32)

    w = weight[...]
    high, low = split_high_low(mixed)
    summed = dot(high, w) + dot(low, w)
    gate = 1.0 / (1.0 + jnp.exp(-summed))
    slope = gate * (1.0 + summed * (1.0 - gate))
    grad = (cot[...].astype(jnp.float32) * slope).astype(jnp.bfloat16)
    grad_all[j] = lax.dot_general(
        grad, w, (((1,), (1,)), ((), ())), preferred_element_type=jnp.float32).astype(jnp.bfloat16)
    gz_copies = []
    for d in order[:-1]:
        gz_copies.append(send(grad_all.at[j], grad_all.at[j], gz_s.at[d - 1], gz_r.at[d - 1],
                              (i, 2 * chip_at(d) + core)))
    gp_copy = send(grad_all.at[j], grad_all.at[j], gp_s.at[0], gp_r.at[0], partner)
    out[...] = (summed * gate).astype(out.dtype)

    mixed_t = mixed.T
    high_t, low_t = split_high_low(mixed_t)
    scale = float(rows * cols * block) ** -0.5
    w_term[...] = (dot(high_t, grad) + dot(low_t, grad)) * scale
    quarter = w_term.shape[0] // rows
    half = quarter // 2

    def quarter_at(index):
        return pl.ds(pl.multiple_of(index * quarter, quarter), quarter)

    w1_copies = []
    for d in range(1, rows):
        w1_copies.append(send(w_term.at[quarter_at(row_at(d))], w_row.at[d - 1], w1_s.at[d - 1], w1_r.at[d - 1],
                              (row_at(d), j)))

    def add_block(source, first):
        term = dot(flipped[:, pl.ds(pl.multiple_of(source * block, block), block)], grad_all[source])
        if first:
            acc[...] = term
        else:
            acc[...] += term

    add_block(j, True)
    gp_copy.wait_recv()
    add_block(2 * q + other, False)

    total = w_term[quarter_at(i)]
    for d, copy in enumerate(w1_copies):
        copy.wait_recv()
        total = total + w_row[d]
    w_quarter[...] = total
    w2_copy = send(w_quarter.at[pl.ds(pl.multiple_of(other * half, half), half)], w_pair, w2_s.at[0], w2_r.at[0],
                   partner)
    started += gz_copies + [gp_copy] + w1_copies + [w2_copy]

    gf_copies = []
    w3_copies = []

    def second_weight_step():
        w2_copy.wait_recv()
        w_hop[q] = w_quarter[pl.ds(pl.multiple_of(core * half, half), half)] + w_pair[...]
        for d in range(1, chips):
            w3_copies.append(send(w_hop.at[q], w_hop.at[q], w3_s.at[d - 1], w3_r.at[d - 1],
                                  (i, 2 * chip_at(d) + core)))

    for d in range(1, chips):
        source = lax.rem(q - d + chips, chips)
        gz_copies[d - 1].wait_recv()
        source_at = 2 * source + core
        gf_copies.append(send(grad_all.at[source_at], grad_all.at[source_at], gf_s.at[d - 1], gf_r.at[d - 1],
                              partner))
        add_block(source_at, False)
        if d == 1:
            second_weight_step()
        gf_copies[d - 1].wait_recv()
        add_block(2 * source + other, False)
    started += gf_copies + w3_copies

    row_copies = []
    for d in range(1, rows):
        at = pl.ds(pl.multiple_of(row_at(d) * block, block), block)
        row_send[d - 1] = acc[at, :].astype(jnp.bfloat16)
        row_copies.append(send(row_send.at[d - 1], row_recv.at[d - 1], row_s.at[d - 1], row_r.at[d - 1],
                               (row_at(d), j)))
    started += row_copies

    for copy in w3_copies:
        copy.wait_recv()
    piece = w_hop[0]
    for k in range(1, chips):
        piece = piece + w_hop[k]
    mine_at = 2 * i + core
    w_all[mine_at] = piece
    w4_copies = []
    for d in range(1, 2 * rows):
        target = (row_at(d // 2), 2 * q + (core if d % 2 == 0 else other))
        w4_copies.append(send(w_all.at[mine_at], w_all.at[mine_at], w4_s.at[d - 1], w4_r.at[d - 1], target))
    started += w4_copies

    final = acc[own_block, :]
    for d, copy in enumerate(row_copies):
        copy.wait_recv()
        final = final + row_recv[d].astype(jnp.float32)
    grad_feat[...] = final.astype(grad_feat.dtype)

    for copy in w4_copies:
        copy.wait_recv()
    grad_weight[...] = w_all[...].reshape(grad_weight.shape)
    for copy in started:
        copy.wait_send()


def local(features, weight, cotangent, tile_values, tile_rows, tile_cols, tile_counts):
    rows = lax.axis_size("row")
    cols = lax.axis_size("col")
    chips = cols // 2
    block, width = features.shape
    hidden = weight.shape[1]
    slot_total, tile = tile_values.shape[2], tile_values.shape[3]
    row_tiles = cols * block // tile
    col_tiles = rows * block // tile
    live = lax.broadcasted_iota(jnp.int32, (slot_total, 1), 0)
    cell = (tile_rows[0, 0] * col_tiles + tile_cols[0, 0])[:, None]
    cells = lax.broadcasted_iota(jnp.int32, (1, row_tiles * col_tiles), 1)
    hit = (cell == cells) & (live < tile_counts[0, 0])
    slot_of = jnp.min(jnp.where(hit, live, slot_total), axis=0)

    half = width // rows // 2
    bf16, f32 = jnp.bfloat16, jnp.float32
    dma = pltpu.SemaphoreType.DMA
    v, any_space = pltpu.VMEM, pl.ANY
    sizes = (block, tile, row_tiles, col_tiles, slot_total)
    scratch = [
        v((slot_total + 1, tile, tile), bf16),
        v((row_tiles * tile, col_tiles * tile), bf16),
        v((col_tiles * tile, row_tiles * tile), bf16),
        v((rows * block, width), bf16),
        v((chips, block, width), bf16),
        v((chips, block, width), bf16),
        v((block, width), f32),
        v((chips - 1, block, width), bf16),
        v((chips - 1, block, width), bf16),
        v((cols, block, width), bf16),
        v((rows * block, width), f32),
        v((rows - 1, block, width), bf16),
        v((rows - 1, block, width), bf16),
        v((width, hidden), f32),
        v((rows - 1, 2 * half, hidden), f32),
        v((2 * half, hidden), f32),
        v((half, hidden), f32),
        v((chips, half, hidden), f32),
        v((2 * rows, half, hidden), f32),
        dma((2,)),
    ]
    for count in (rows - 1, chips, chips - 1, 1, chips - 1, chips - 1, rows - 1, rows - 1, 1, chips - 1,
                  2 * rows - 1):
        scratch += [dma((count,)), dma((count,))]
    vmem = pl.BlockSpec(memory_space=pltpu.VMEM)
    hbm = pl.BlockSpec(memory_space=any_space)
    return pl.pallas_call(
        functools.partial(kernel, rows, cols, sizes),
        out_shape=(
            jax.ShapeDtypeStruct((block, hidden), bf16),
            jax.ShapeDtypeStruct((block, width), bf16),
            jax.ShapeDtypeStruct((width, hidden), f32),
        ),
        in_specs=[pl.BlockSpec(memory_space=pltpu.SMEM), hbm, vmem, vmem, hbm],
        out_specs=(vmem, vmem, vmem),
        scratch_shapes=scratch,
        compiler_params=pltpu.CompilerParams(collective_id=0, has_side_effects=True),
    )(slot_of, features, weight, cotangent, tile_values[0, 0])


def solution(mesh):
    placed = (
        P(("row", "col"), None),
        P(),
        P(("row", "col"), None),
        P("row", "col", None, None, None),
        P("row", "col", None),
        P("row", "col", None),
        P("row", "col"),
    )
    return jax.shard_map(
        local,
        mesh=mesh,
        in_specs=placed,
        out_specs=(P(("row", "col"), None), P(("row", "col"), None), P()),
        check_vma=False,
    )
```

```python
import functools

import jax
import jax.numpy as jnp
from jax import lax
from jax.experimental import pallas as pl
from jax.experimental.pallas import tpu as pltpu
from jax.sharding import PartitionSpec as P

MESH = pl.DeviceIdType.MESH


def dot(a, b):
    return jnp.dot(a, b, preferred_element_type=jnp.float32)


def split_high_low(values):
    high = values.astype(jnp.bfloat16)
    return high, (values - high.astype(jnp.float32)).astype(jnp.bfloat16)


def finish(*refs):
    count = len(refs) // 2
    for source, result in zip(refs[:count], refs[count:]):
        result[...] = source[...]


def kernel(rows, cols, sizes, live_count, tile_row, tile_col, feats, weight, cot, tiles, out, grad_feat, grad_weight,
           keys, table, slot_of, summing, slots, dense, flipped, feat_all, pair_send, pair_recv, pair_own, hop_send, hop_recv,
           grad_all, acc, row_send, row_recv, w_term, w_row, w_quarter, w_pair, w_hop, w_all,
           load_sem, feat_s, feat_r, pair_s, pair_r, hop_s, hop_r, gp_s, gp_r, gz_s, gz_r, gf_s, gf_r,
           row_s, row_r, w1_s, w1_r, w2_s, w2_r, w3_s, w3_r, w4_s, w4_r):
    block, tile, row_tiles, col_tiles, slot_total = sizes
    chips = cols // 2
    i = lax.axis_index("row")
    j = lax.axis_index("col")
    q = j // 2
    core = j % 2
    other = 1 - core
    partner = (i, 2 * q + other)

    def row_at(step):
        return lax.rem(i + step, rows)

    def chip_at(step):
        if chips & (chips - 1):
            return lax.rem(chips + step - q, chips)
        paired, bit = q, 1
        while bit <= step:
            if step & bit:
                paired = paired + bit - 2 * bit * ((q // bit) % 2)
            bit *= 2
        return paired

    def send(src, dst, ssem, rsem, device):
        copy = pltpu.make_async_remote_copy(
            src_ref=src, dst_ref=dst, send_sem=ssem, recv_sem=rsem, device_id=device, device_id_type=MESH)
        copy.start()
        return copy

    started = []

    load_tiles = pltpu.make_async_copy(tiles, slots.at[pl.ds(0, slot_total)], load_sem.at[0])
    load_tiles.start()
    own_block = pl.ds(pl.multiple_of(i * block, block), block)
    load_feats = pltpu.make_async_copy(feats, feat_all.at[own_block], load_sem.at[1])
    load_feats.start()

    barrier = pltpu.get_barrier_semaphore()
    peers = [partner]
    for d in range(1, rows):
        peers.append((row_at(d), j))
        peers.append((row_at(d), 2 * q + other))
    for d in range(1, chips):
        peers.append((i, 2 * chip_at(d) + core))
    for peer in peers:
        pl.semaphore_signal(barrier, inc=1, device_id=peer, device_id_type=MESH)

    cell_total = row_tiles * col_tiles
    lanes = lax.broadcasted_iota(jnp.int32, (1, slot_total), 1)
    keys[...] = jnp.full(keys.shape, -1, jnp.int32)
    keys[:, :slot_total] = jnp.where(lanes < live_count[0, 0], tile_row[...] * col_tiles + tile_col[...], -1)
    padded = keys.shape[1]
    key_columns = jnp.broadcast_to(keys[...], (128, padded)).T
    slot_ids = lax.broadcasted_iota(jnp.int32, (padded, 128), 0) - slot_total
    cell_ids = lax.broadcasted_iota(jnp.int32, (padded, 128), 1)
    for first in range(0, cell_total, 128):
        found = jnp.where(key_columns == cell_ids + first, slot_ids, 0)
        table[:, first:first + 128] = jnp.sum(found, axis=0, keepdims=True) + slot_total
    load_table = pltpu.make_async_copy(table, slot_of, load_sem.at[2])
    load_table.start()
    slots[slot_total] = jnp.zeros((tile, tile), jnp.bfloat16)
    pl.semaphore_wait(barrier, len(peers))

    feat_copies = []
    for d in range(1, rows):
        feat_copies.append(send(feats, feat_all.at[own_block], feat_s.at[d - 1], feat_r.at[d - 1], (row_at(d), j)))

    load_table.wait()
    load_tiles.wait()

    def place(r, carry):
        at = pl.ds(pl.multiple_of(r * tile, tile), tile)
        for c in range(col_tiles):
            dense[at, c * tile:(c + 1) * tile] = slots[slot_of[0, r * col_tiles + c]]
        return carry

    lax.fori_loop(0, row_tiles, place, 0)

    def product_at(at, source):
        source_at = pl.ds(pl.multiple_of(source * block, block), block)
        return dot(dense[at, source_at], feat_all[source_at, :])

    load_feats.wait()
    for d in range(rows - 1):
        if d:
            feat_copies[d - 1].wait_recv()
        source = lax.rem(i - d + rows, rows)

        def add_source(dest, carry):
            at = pl.ds(pl.multiple_of(dest * block, block), block)
            if d:
                summing[at, :] += product_at(at, source)
            else:
                summing[at, :] = product_at(at, source)
            return carry

        lax.fori_loop(0, cols, add_source, 0)
    feat_copies[rows - 2].wait_recv()
    last = lax.rem(i + 1, rows)

    def partial_of(dest):
        at = pl.ds(pl.multiple_of(dest * block, block), block)
        return summing[at, :] + product_at(at, last)

    started += feat_copies
    order = list(range(chips - 1, -1, -1))
    pair_copies = {}
    for d in order:
        pair_send[d] = partial_of(2 * chip_at(d) + other).astype(jnp.bfloat16)
        pair_copies[d] = send(pair_send.at[d], pair_recv.at[d], pair_s.at[d], pair_r.at[d], partner)
    hop_copies = {}
    for d in order:
        mine = partial_of(2 * chip_at(d) + core)
        pair_copies[d].wait_recv()
        mine = mine + pair_recv[d].astype(jnp.float32)
        if d:
            hop_send[d - 1] = mine.astype(jnp.bfloat16)
            hop_copies[d] = send(hop_send.at[d - 1], hop_recv.at[d - 1], hop_s.at[d - 1], hop_r.at[d - 1],
                                 (i, 2 * chip_at(d) + core))
        else:
            pair_own[...] = mine
    started += list(pair_copies.values()) + list(hop_copies.values())

    def turn(r, carry):
        at = pl.ds(pl.multiple_of(r * tile, tile), tile)
        for c in range(col_tiles):
            flipped[c * tile:(c + 1) * tile, at] = dense[at, c * tile:(c + 1) * tile].T
        return carry

    lax.fori_loop(0, row_tiles, turn, 0)

    mixed = pair_own[...]
    for d in range(1, chips):
        hop_copies[d].wait_recv()
        mixed = mixed + hop_recv[d - 1].astype(jnp.float32)

    w = weight[...]
    high, low = split_high_low(mixed)
    summed = dot(high, w) + dot(low, w)
    gate = 1.0 / (1.0 + jnp.exp(-summed))
    slope = gate * (1.0 + summed * (1.0 - gate))
    grad = (cot[...].astype(jnp.float32) * slope).astype(jnp.bfloat16)
    grad_all[j] = lax.dot_general(
        grad, w, (((1,), (1,)), ((), ())), preferred_element_type=jnp.float32).astype(jnp.bfloat16)
    gz_copies = {}
    for d in order[:-1]:
        gz_copies[d] = send(grad_all.at[j], grad_all.at[j], gz_s.at[d - 1], gz_r.at[d - 1],
                            (i, 2 * chip_at(d) + core))
    gp_copy = send(grad_all.at[j], grad_all.at[j], gp_s.at[0], gp_r.at[0], partner)
    out[...] = (summed * gate).astype(out.dtype)

    mixed_t = mixed.T
    high_t, low_t = split_high_low(mixed_t)
    scale = float(rows * cols * block) ** -0.5
    w_term[...] = (dot(high_t, grad) + dot(low_t, grad)) * scale
    quarter = w_term.shape[0] // rows
    half = quarter // 2

    def quarter_at(index):
        return pl.ds(pl.multiple_of(index * quarter, quarter), quarter)

    w1_copies = []
    for d in range(1, rows):
        w1_copies.append(send(w_term.at[quarter_at(row_at(d))], w_row.at[d - 1], w1_s.at[d - 1], w1_r.at[d - 1],
                              (row_at(d), j)))

    def add_block(source, first):
        term = dot(flipped[:, pl.ds(pl.multiple_of(source * block, block), block)], grad_all[source])
        if first:
            acc[...] = term
        else:
            acc[...] += term

    add_block(j, True)
    gp_copy.wait_recv()
    add_block(2 * q + other, False)

    total = w_term[quarter_at(i)]
    for d, copy in enumerate(w1_copies):
        copy.wait_recv()
        total = total + w_row[d]
    w_quarter[...] = total
    w2_copy = send(w_quarter.at[pl.ds(pl.multiple_of(other * half, half), half)], w_pair, w2_s.at[0], w2_r.at[0],
                   partner)
    started += list(gz_copies.values()) + [gp_copy] + w1_copies + [w2_copy]

    gf_copies = []
    w3_copies = []

    def second_weight_step():
        w2_copy.wait_recv()
        w_hop[q] = w_quarter[pl.ds(pl.multiple_of(core * half, half), half)] + w_pair[...]
        for d in range(1, chips):
            w3_copies.append(send(w_hop.at[q], w_hop.at[q], w3_s.at[d - 1], w3_r.at[d - 1],
                                  (i, 2 * chip_at(d) + core)))

    for d in range(1, chips):
        source = chip_at(d)
        gz_copies[d].wait_recv()
        source_at = 2 * source + core
        gf_copies.append(send(grad_all.at[source_at], grad_all.at[source_at], gf_s.at[d - 1], gf_r.at[d - 1],
                              partner))
        add_block(source_at, False)
        if d == 1:
            second_weight_step()
        gf_copies[d - 1].wait_recv()
        add_block(2 * source + other, False)
    started += gf_copies + w3_copies

    row_copies = []
    for d in range(1, rows):
        at = pl.ds(pl.multiple_of(row_at(d) * block, block), block)
        row_send[d - 1] = acc[at, :].astype(jnp.bfloat16)
        row_copies.append(send(row_send.at[d - 1], row_recv.at[d - 1], row_s.at[d - 1], row_r.at[d - 1],
                               (row_at(d), j)))
    started += row_copies

    for copy in w3_copies:
        copy.wait_recv()
    piece = w_hop[0]
    for k in range(1, chips):
        piece = piece + w_hop[k]
    mine_at = 2 * i + core
    w_all[mine_at] = piece
    w4_copies = []
    for d in range(1, 2 * rows):
        target = (row_at(d // 2), 2 * q + (core if d % 2 == 0 else other))
        w4_copies.append(send(w_all.at[mine_at], w_all.at[mine_at], w4_s.at[d - 1], w4_r.at[d - 1], target))
    started += w4_copies

    final = acc[own_block, :]
    for d, copy in enumerate(row_copies):
        copy.wait_recv()
        final = final + row_recv[d].astype(jnp.float32)
    grad_feat[...] = final.astype(grad_feat.dtype)

    for copy in w4_copies:
        copy.wait_recv()
    grad_weight[...] = w_all[...].reshape(grad_weight.shape)
    for copy in started:
        copy.wait_send()


def local(features, weight, cotangent, tile_values, tile_rows, tile_cols, tile_counts):
    rows = lax.axis_size("row")
    cols = lax.axis_size("col")
    chips = cols // 2
    block, width = features.shape
    hidden = weight.shape[1]
    slot_total, tile = tile_values.shape[2], tile_values.shape[3]
    row_tiles = cols * block // tile
    col_tiles = rows * block // tile
    cell_total = row_tiles * col_tiles
    half = width // rows // 2
    bf16, f32 = jnp.bfloat16, jnp.float32
    dma = pltpu.SemaphoreType.DMA
    v, any_space = pltpu.VMEM, pl.ANY
    sizes = (block, tile, row_tiles, col_tiles, slot_total)
    scratch = [
        v((1, pl.cdiv(slot_total, 128) * 128), jnp.int32),
        v((1, cell_total), jnp.int32),
        pltpu.SMEM((1, cell_total), jnp.int32),
        v((row_tiles * tile, width), f32),
        v((slot_total + 1, tile, tile), bf16),
        v((row_tiles * tile, col_tiles * tile), bf16),
        v((col_tiles * tile, row_tiles * tile), bf16),
        v((rows * block, width), bf16),
        v((chips, block, width), bf16),
        v((chips, block, width), bf16),
        v((block, width), f32),
        v((chips - 1, block, width), bf16),
        v((chips - 1, block, width), bf16),
        v((cols, block, width), bf16),
        v((rows * block, width), f32),
        v((rows - 1, block, width), bf16),
        v((rows - 1, block, width), bf16),
        v((width, hidden), f32),
        v((rows - 1, 2 * half, hidden), f32),
        v((2 * half, hidden), f32),
        v((half, hidden), f32),
        v((chips, half, hidden), f32),
        v((2 * rows, half, hidden), f32),
        dma((3,)),
    ]
    for count in (rows - 1, chips, chips - 1, 1, chips - 1, chips - 1, rows - 1, rows - 1, 1, chips - 1,
                  2 * rows - 1):
        scratch += [dma((count,)), dma((count,))]
    vmem = pl.BlockSpec(memory_space=pltpu.VMEM)
    hbm = pl.BlockSpec(memory_space=any_space)
    results = (
        jax.ShapeDtypeStruct((block, hidden), bf16),
        jax.ShapeDtypeStruct((block, width), bf16),
        jax.ShapeDtypeStruct((width, hidden), f32),
    )
    values = pl.pallas_call(
        functools.partial(kernel, rows, cols, sizes),
        out_shape=results,
        in_specs=[pl.BlockSpec(memory_space=pltpu.SMEM), vmem, vmem, hbm, vmem, vmem, hbm],
        out_specs=(vmem, vmem, vmem),
        scratch_shapes=scratch,
        compiler_params=pltpu.CompilerParams(collective_id=0, has_side_effects=True),
    )(tile_counts, tile_rows[0], tile_cols[0], features, weight, cotangent, tile_values[0, 0])
    return pl.pallas_call(
        finish,
        out_shape=results,
        in_specs=[vmem] * 3,
        out_specs=(vmem, vmem, vmem),
    )(*values)


def solution(mesh):
    placed = (
        P(("row", "col"), None),
        P(),
        P(("row", "col"), None),
        P("row", "col", None, None, None),
        P("row", "col", None),
        P("row", "col", None),
        P("row", "col"),
    )
    return jax.shard_map(
        local,
        mesh=mesh,
        in_specs=placed,
        out_specs=(P(("row", "col"), None), P(("row", "col"), None), P()),
        check_vma=False,
    )
```
